32 devices in a mesh: seq: 4 (over y, x), fsdp: 8 (over z, core).
Axes of the slice: x: 2, y: 2, z: 4, core: 2. Of those that a mesh axis runs over, the one named last changes fastest.
Arguments:
- layer_input: bfloat16 [8, 512, 1024], P('fsdp', 'seq'), may hold values from -6 to 6
- attn_gain: bfloat16 [1024], P('fsdp'), may hold values from 0.5 to 1.5
- qkv_weight: bfloat16 [3072, 1024], P('fsdp'), may hold values from -2 to 2
- out_weight: bfloat16 [1024, 1024], P('fsdp'), may hold values from -4 to 4
- mlp_gain: bfloat16 [1024], P('fsdp'), may hold values from 0.5 to 1.5
- input_weight: bfloat16 [2624, 1024], P('fsdp'), may hold values from -0.1875 to 0.1875
- gate_weight: bfloat16 [2624, 1024], P('fsdp'), may hold values from -0.1875 to 0.1875
- down_weight: bfloat16 [1024, 2624], P('fsdp'), may hold values from -0.125 to 0.125
- out_grad: bfloat16 [8, 512, 1024], P('fsdp', 'seq'), may hold values from -6 to 6
Outputs:
- layer_output: bfloat16 [8, 512, 1024], P('fsdp', 'seq')
- input_grad: float32 [8, 512, 1024], P('fsdp', 'seq')
- attn_gain_grad: float32 [1024], P('fsdp')
- qkv_weight_grad: float32 [3072, 1024], P('fsdp')
- out_weight_grad: float32 [1024, 1024], P('fsdp')
- mlp_gain_grad: float32 [1024], P('fsdp')
- input_weight_grad: float32 [2624, 1024], P('fsdp')
- gate_weight_grad: float32 [2624, 1024], P('fsdp')
- down_weight_grad: float32 [1024, 2624], P('fsdp')
The draws below stay inside these ranges and needn't reach their ends.
All inputs are finite; a program needn't handle non-finite values.
Results may differ from the reference program's by a relative error of at most 0.02.
Values may be sent and summed in bfloat16 or wider, within the bound.
A program may use at most 192 MiB of HBM per device.

```python
import math
import jax
import jax.numpy as jnp
from jax import lax

D = 1024
H = 16
HD = 64
FF = 2624
LENGTH = 512
BATCH = 8


def draw_qkv_weight(key, part):
    first_key = jax.random.fold_in(key, 11)
    base = jax.random.normal(first_key, (3 * D, D), jnp.float32) * D ** (-0.5)
    whole = base
    return jnp.clip(whole, -2.0, 2.0).astype(jnp.bfloat16)


def strengthened(result, stream_key, source, target, parts, factor):
    def block_of(position):
        return (jnp.arange(result.shape[position]) // (result.shape[position] // parts)).reshape((-1,) + (1,) * (result.ndim - 1 - position))

    one_side = jax.random.permutation(stream_key, parts)[block_of(target)]
    other_side = (block_of(target) + parts // 2) % parts
    return jnp.where((block_of(source) == one_side) | (block_of(source) == other_side), factor * result, result)


def block_levels(rng, shape, pieces, low, high):
    def one(position, parts):
        heights = jax.random.uniform(jax.random.fold_in(jax.random.fold_in(rng, 6), position), (parts,), jnp.float32, low / len(pieces), high / len(pieces))
        return jnp.repeat(jnp.exp(heights), shape[position] // parts).reshape((-1,) + (1,) * (len(shape) - position - 1))

    level = one(*pieces[0])
    for cut in pieces[1:]:
        level = level * one(*cut)
    return level


def bell_draw(stream_key, extent, deviation, limit, pieces=(), kind=jnp.bfloat16):
    entries = deviation * jax.random.normal(stream_key, extent, jnp.float32)
    if pieces:
        entries = entries * block_levels(stream_key, extent, pieces, -0.22, 0.18)
    return jnp.clip(entries, -limit, limit).astype(kind)


def bell_draw_with(rng, dims, spread, limit, shards, heavy, kind=jnp.bfloat16):
    entries = spread * jax.random.normal(rng, dims, jnp.float32)
    if shards:
        entries = entries * block_levels(rng, dims, shards, -0.22, 0.18)
    return jnp.clip(strengthened(entries, jax.random.fold_in(rng, 3), *heavy), -limit, limit).astype(kind)


def setup_inputs(seed: int = 0) -> dict:
    streams_of = jax.random.split(jax.random.key(seed), 10)
    layer_input = bell_draw(streams_of[0], (BATCH, LENGTH, D), 1.0, 6.0, ((0, 8), (1, 4)))
    attn_gain = jnp.clip(1.0 + 0.1 * jax.random.normal(streams_of[1], (D,), jnp.float32), 0.5, 1.5).astype(jnp.bfloat16)
    qkv_weight = draw_qkv_weight(jax.random.fold_in(streams_of[9], 71), 0)
    out_weight = bell_draw(streams_of[3], (D, D), (max(1, D // LENGTH)) ** -0.5, 4.0, ((0, 8),))
    mlp_gain = jnp.clip(1.0 + 0.1 * jax.random.normal(streams_of[4], (D,), jnp.float32), 0.5, 1.5).astype(jnp.bfloat16)
    input_weight = bell_draw(streams_of[5], (FF, D), D ** -0.5, 0.1875, ((0, 8),))
    gate_weight = bell_draw(streams_of[6], (FF, D), D ** -0.5, 0.1875, ((0, 8),))
    down_weight = bell_draw(streams_of[7], (D, FF), FF ** -0.5, 0.125, ((0, 8),))
    out_grad = bell_draw_with(streams_of[8], (BATCH, LENGTH, D), 1.0, 6.0, ((0, 8), (1, 4)), (0, 2, 8, 2.0))
    return {"layer_input": layer_input, "attn_gain": attn_gain, "qkv_weight": qkv_weight, "out_weight": out_weight, "mlp_gain": mlp_gain, "input_weight": input_weight, "gate_weight": gate_weight, "down_weight": down_weight, "out_grad": out_grad}


EPSILON = 1e-05
THETA = 160000.0
SQRT_HALF = 0.7071067811865476
INV_SQRT_TWO_PI = 0.3989422804014327

def product_t(left, right):
    return lax.dot_general(left, right, (((1,), (1,)), ((), ())), preferred_element_type=jnp.float32)

def product_tn(left, right):
    return lax.dot_general(left, right, (((0,), (0,)), ((), ())), preferred_element_type=jnp.float32)

def norm_forward(values, gain):
    row_mean = lax.optimization_barrier(jnp.mean(values, -1, keepdims=True))
    centred = values - row_mean
    inv_std = lax.rsqrt(lax.optimization_barrier(jnp.mean(centred * centred, -1, keepdims=True)) + EPSILON)
    unit = centred * inv_std
    return ((unit * gain.astype(jnp.float32)).astype(jnp.bfloat16), unit, inv_std)

def norm_backward(grad_out, unit, inv_std, gain):
    scaled = grad_out * gain.astype(jnp.float32)
    grad_in = inv_std * (scaled - lax.optimization_barrier(jnp.mean(scaled, -1, keepdims=True)) - unit * lax.optimization_barrier(jnp.mean(scaled * unit, -1, keepdims=True)))
    return (grad_in, lax.optimization_barrier(jnp.sum(grad_out * unit, 0)))

def rotary_tables(positions, head_dim):
    half_dim = head_dim // 2
    inverse = jnp.power(THETA, -(jnp.arange(half_dim, dtype=jnp.float32) * (2.0 / head_dim)))
    angles = positions.astype(jnp.float32)[:, None] * inverse[None, :]
    angles = jnp.concatenate([angles, angles], -1)
    return (jnp.cos(angles), jnp.sin(angles))

def rotate(values, cosine, sine):
    half_dim = values.shape[-1] // 2
    turned = jnp.concatenate([-values[..., half_dim:], values[..., :half_dim]], -1)
    return values * cosine[:, None, :] + turned * sine[:, None, :]

def unrotate(grads, cosine, sine):
    half_dim = grads.shape[-1] // 2
    scaled = grads * sine[:, None, :]
    back = jnp.concatenate([scaled[..., half_dim:], -scaled[..., :half_dim]], -1)
    return grads * cosine[:, None, :] + back

def gelu_value(values):
    return 0.5 * values * (1.0 + lax.erf(values * SQRT_HALF))

def gelu_slope(values):
    return 0.5 * (1.0 + lax.erf(values * SQRT_HALF)) + values * jnp.exp(-0.5 * values * values) * INV_SQRT_TWO_PI

def one_sequence(tokens_in, grad_low, weights):
    qkv_w, out_w, in_w, gate_w, down_w, attn_g, mlp_g = weights
    head_scale = 1.0 / math.sqrt(HD)
    tokens = tokens_in.astype(jnp.float32)
    attn_normed, attn_unit, attn_rstd = norm_forward(tokens, attn_g)
    qkv = product_t(attn_normed, qkv_w)
    cosine, sine = rotary_tables(jnp.arange(LENGTH, dtype=jnp.int32), HD)
    query = rotate(qkv[:, :D].reshape(LENGTH, H, HD), cosine, sine).astype(jnp.bfloat16)
    keys = rotate(qkv[:, D:2 * D].reshape(LENGTH, H, HD), cosine, sine).astype(jnp.bfloat16)
    values = qkv[:, 2 * D:].reshape(LENGTH, H, HD).astype(jnp.bfloat16)
    query_f = query.astype(jnp.float32)
    keys_f = keys.astype(jnp.float32)
    values_f = values.astype(jnp.float32)
    scores = jnp.einsum('qhd,khd->hqk', query_f, keys_f) * head_scale
    row_top = lax.optimization_barrier(jnp.max(scores, -1, keepdims=True))
    log_total = row_top + jnp.log(lax.optimization_barrier(jnp.sum(jnp.exp(scores - row_top), -1, keepdims=True)))
    probs_full = jnp.exp(scores - log_total)
    probs = probs_full.astype(jnp.bfloat16)
    attended = jnp.einsum('hqk,khd->qhd', probs.astype(jnp.float32), values_f).astype(jnp.bfloat16).reshape(LENGTH, D)
    resid = tokens + product_t(attended, out_w)
    mlp_normed, mlp_unit, mlp_rstd = norm_forward(resid, mlp_g)
    upper = product_t(mlp_normed, in_w)
    gating = product_t(mlp_normed, gate_w)
    hidden = (gelu_value(upper) * gating).astype(jnp.bfloat16)
    output = (resid + product_t(hidden, down_w)).astype(jnp.bfloat16)
    grad_out = grad_low.astype(jnp.float32)
    down_grad = product_tn(grad_low, hidden)
    hidden_grad = jnp.dot(grad_low, down_w, preferred_element_type=jnp.float32)
    upper_grad = (hidden_grad * gating * gelu_slope(upper)).astype(jnp.bfloat16)
    gating_grad = (hidden_grad * gelu_value(upper)).astype(jnp.bfloat16)
    in_grad = product_tn(upper_grad, mlp_normed)
    gate_grad = product_tn(gating_grad, mlp_normed)
    mlp_normed_grad = jnp.dot(upper_grad, in_w, preferred_element_type=jnp.float32) + jnp.dot(gating_grad, gate_w, preferred_element_type=jnp.float32)
    resid_part, mlp_gain_grad = norm_backward(mlp_normed_grad, mlp_unit, mlp_rstd, mlp_g)
    resid_grad = grad_out + resid_part
    resid_low = resid_grad.astype(jnp.bfloat16)
    out_grad_w = product_tn(resid_low, attended)
    attended_grad = jnp.dot(resid_low, out_w, preferred_element_type=jnp.float32).astype(jnp.bfloat16)
    grad_heads = attended_grad.reshape(LENGTH, H, HD).astype(jnp.float32)
    delta = lax.optimization_barrier(jnp.sum(grad_heads * attended.reshape(LENGTH, H, HD).astype(jnp.float32), -1)).T
    value_grad = jnp.einsum('hqk,qhd->khd', probs.astype(jnp.float32), grad_heads).astype(jnp.bfloat16)
    prob_grad = jnp.einsum('qhd,khd->hqk', grad_heads, values_f)
    score_grad = (probs_full * (prob_grad - delta[..., None]) * head_scale).astype(jnp.bfloat16).astype(jnp.float32)
    query_grad = jnp.einsum('hqk,khd->qhd', score_grad, keys_f).astype(jnp.bfloat16)
    key_grad = jnp.einsum('hqk,qhd->khd', score_grad, query_f).astype(jnp.bfloat16)
    query_back = unrotate(query_grad.astype(jnp.float32), cosine, sine).astype(jnp.bfloat16).reshape(LENGTH, D)
    key_back = unrotate(key_grad.astype(jnp.float32), cosine, sine).astype(jnp.bfloat16).reshape(LENGTH, D)
    qkv_grad = jnp.concatenate([query_back, key_back, value_grad.reshape(LENGTH, D)], 1)
    qkv_grad_w = product_tn(qkv_grad, attn_normed)
    attn_normed_grad = jnp.dot(qkv_grad, qkv_w, preferred_element_type=jnp.float32)
    input_part, attn_gain_grad = norm_backward(attn_normed_grad, attn_unit, attn_rstd, attn_g)
    input_grad = resid_grad + input_part
    grads = (qkv_grad_w, out_grad_w, in_grad, gate_grad, down_grad, attn_gain_grad, mlp_gain_grad)
    return (output, input_grad, grads)

def reference(layer_input, attn_gain, qkv_weight, out_weight, mlp_gain, input_weight, gate_weight, down_weight, out_grad):
    weights = (qkv_weight, out_weight, input_weight, gate_weight, down_weight, attn_gain, mlp_gain)

    def step(totals, pair):
        output, input_grad, grads = one_sequence(pair[0], pair[1], weights)
        return (jax.tree.map(jnp.add, totals, grads), (output, input_grad))
    zeros = (jnp.zeros((3 * D, D), jnp.float32), jnp.zeros((D, D), jnp.float32), jnp.zeros((FF, D), jnp.float32), jnp.zeros((FF, D), jnp.float32), jnp.zeros((D, FF), jnp.float32), jnp.zeros((D,), jnp.float32), jnp.zeros((D,), jnp.float32))
    totals, (outputs, input_grads) = lax.scan(step, zeros, (layer_input, out_grad))
    return (outputs, input_grads, totals[5], totals[0], totals[1], totals[6], totals[2], totals[3], totals[4])
```

```python
import math

import jax
import jax.numpy as jnp
from jax import lax
from jax.sharding import PartitionSpec as P

D = 1024
H = 16
HD = 64


EPSILON = 1e-05
THETA = 160000.0
SQRT_HALF = 0.7071067811865476
INV_SQRT_TWO_PI = 0.3989422804014327


def product_t(left, right):
    return lax.dot_general(
        left, right, (((1,), (1,)), ((), ())), preferred_element_type=jnp.float32
    )


def product_tn(left, right):
    return lax.dot_general(
        left, right, (((0,), (0,)), ((), ())), preferred_element_type=jnp.float32
    )


def norm_forward(values, gain):
    row_mean = jnp.mean(values, -1, keepdims=True)
    centred = values - row_mean
    inv_std = lax.rsqrt(jnp.mean(centred * centred, -1, keepdims=True) + EPSILON)
    unit = centred * inv_std
    return ((unit * gain.astype(jnp.float32)).astype(jnp.bfloat16), unit, inv_std)


def norm_backward(grad_out, unit, inv_std, gain):
    scaled = grad_out * gain.astype(jnp.float32)
    grad_in = inv_std * (
        scaled
        - jnp.mean(scaled, -1, keepdims=True)
        - unit * jnp.mean(scaled * unit, -1, keepdims=True)
    )
    return (grad_in, jnp.sum(grad_out * unit, 0))


def rotary_tables(positions, head_dim):
    half_dim = head_dim // 2
    inverse = jnp.power(THETA, -(jnp.arange(half_dim, dtype=jnp.float32) * (2.0 / head_dim)))
    angles = positions.astype(jnp.float32)[:, None] * inverse[None, :]
    angles = jnp.concatenate([angles, angles], -1)
    return (jnp.cos(angles), jnp.sin(angles))


def rotate(values, cosine, sine):
    half_dim = values.shape[-1] // 2
    turned = jnp.concatenate([-values[..., half_dim:], values[..., :half_dim]], -1)
    return values * cosine[:, None, :] + turned * sine[:, None, :]


def unrotate(grads, cosine, sine):
    half_dim = grads.shape[-1] // 2
    scaled = grads * sine[:, None, :]
    back = jnp.concatenate([scaled[..., half_dim:], -scaled[..., :half_dim]], -1)
    return grads * cosine[:, None, :] + back


def gelu_value(values):
    return 0.5 * values * (1.0 + lax.erf(values * SQRT_HALF))


def gelu_slope(values):
    return (
        0.5 * (1.0 + lax.erf(values * SQRT_HALF))
        + values * jnp.exp(-0.5 * values * values) * INV_SQRT_TWO_PI
    )


def ring_send(value, axis, step, stride=1):
    size = lax.axis_size(axis) // stride
    pairs = [
        (i * stride + j, ((i + step) % size) * stride + j)
        for i in range(size)
        for j in range(stride)
    ]
    return lax.ppermute(value, axis, pairs)


def swap_cores(value):
    size = lax.axis_size("fsdp")
    return lax.ppermute(value, "fsdp", [(i, i ^ 1) for i in range(size)])


def place_parts(parts, position, axis):
    size = len(parts)
    width = parts[0].shape[axis]
    rising = parts[::-1]
    twice = jnp.concatenate(rising + rising[:-1], axis)
    return lax.dynamic_slice_in_dim(twice, (size - 1 - position) * width, size * width, axis)


def take_block(value, index, count, axis):
    width = value.shape[axis] // count
    return lax.dynamic_slice_in_dim(value, index * width, width, axis)


def gather_weight(shard, axis):
    groups = lax.axis_size("seq")
    chips = lax.axis_size("fsdp") // 2
    group = lax.axis_index("seq")
    chip, core = lax.axis_index("fsdp") // 2, lax.axis_index("fsdp") % 2
    share = take_block(shard, group, groups, axis)[None]
    column = [share] + [ring_send(share, "fsdp", k, 2) for k in range(1, chips)]
    column = place_parts(column, chip, 0)
    plane = [column] + [ring_send(column, "seq", k) for k in range(1, groups)]
    other = [swap_cores(part) for part in plane]
    mine = place_parts(plane, group, 1 + axis)
    theirs = place_parts(other, group, 1 + axis)
    even = jnp.where(core == 0, mine, theirs)
    odd = jnp.where(core == 0, theirs, mine)
    return jnp.stack([even, odd], 1).reshape((2 * chips,) + shard.shape)


def reduce_weight(grad, axis):
    groups = lax.axis_size("seq")
    owners = grad.shape[0]
    chips = owners // 2
    group = lax.axis_index("seq")
    chip, core = lax.axis_index("fsdp") // 2, lax.axis_index("fsdp") % 2
    pairs = grad.astype(jnp.bfloat16).reshape((chips, 2) + grad.shape[1:])
    keep = lax.dynamic_index_in_dim(pairs, core, 1, False)
    give = lax.dynamic_index_in_dim(pairs, 1 - core, 1, False)
    total = (keep.astype(jnp.float32) + swap_cores(give).astype(jnp.float32)).astype(jnp.bfloat16)
    part = take_block(total, group, groups, 1 + axis).astype(jnp.float32)
    for k in range(1, groups):
        piece = take_block(total, lax.rem(group + k, groups), groups, 1 + axis)
        part = part + ring_send(piece, "seq", k).astype(jnp.float32)
    part = part.astype(jnp.bfloat16)
    share = lax.dynamic_index_in_dim(part, chip, 0, False).astype(jnp.float32)
    for k in range(1, chips):
        piece = lax.dynamic_index_in_dim(part, lax.rem(chip + k, chips), 0, False)
        share = share + ring_send(piece, "fsdp", k, 2).astype(jnp.float32)
    share = share.astype(jnp.bfloat16)
    shares = [share] + [ring_send(share, "seq", k) for k in range(1, groups)]
    return place_parts(shares, group, axis).astype(jnp.float32)


def on_device(
    layer_input,
    attn_gain,
    qkv_weight,
    out_weight,
    mlp_gain,
    input_weight,
    gate_weight,
    down_weight,
    out_grad,
):
    tok_count = layer_input.shape[1]
    tokens_low = layer_input.reshape(tok_count, D)
    groups = lax.axis_size("seq")
    length = groups * tok_count
    local_width = D // groups
    local_heads = local_width // HD
    head_scale = 1.0 / math.sqrt(HD)
    block = min(512, length)
    block_count = length // block
    owners = lax.axis_size("fsdp")
    qkv_rows, out_rows, ff_rows = qkv_weight.shape[0], out_weight.shape[0], input_weight.shape[0]
    gain_rows = attn_gain.shape[0]
    gains = jnp.concatenate([attn_gain, mlp_gain])[None, :]
    gains = jnp.tile(gains, (16, D // gains.shape[1]))
    first = gather_weight(jnp.concatenate([qkv_weight, gains], 0), 1)
    qkv_w = first[:, :qkv_rows].reshape(owners * qkv_rows, D)
    attn_g = first[:, qkv_rows, :gain_rows].reshape(D)
    mlp_g = first[:, qkv_rows, gain_rows : 2 * gain_rows].reshape(D)
    out_w = gather_weight(out_weight, 1).reshape(D, D)
    in_w = gather_weight(input_weight, 1).reshape(owners * ff_rows, D)
    gate_w = gather_weight(gate_weight, 1).reshape(owners * ff_rows, D)
    down_w = gather_weight(down_weight, 0).reshape(D, owners * ff_rows)
    tokens = tokens_low.astype(jnp.float32)
    attn_normed, attn_unit, attn_rstd = norm_forward(tokens, attn_g)
    qkv = product_t(attn_normed, qkv_w)
    positions = lax.axis_index("seq") * tok_count + jnp.arange(tok_count, dtype=jnp.int32)
    cosine, sine = rotary_tables(positions, HD)
    query_rot = (
        rotate(qkv[:, :D].reshape(tok_count, H, HD), cosine, sine)
        .astype(jnp.bfloat16)
        .reshape(tok_count, D)
    )
    key_rot = (
        rotate(qkv[:, D : 2 * D].reshape(tok_count, H, HD), cosine, sine)
        .astype(jnp.bfloat16)
        .reshape(tok_count, D)
    )
    value_low = qkv[:, 2 * D :].astype(jnp.bfloat16)
    packed = jnp.stack([query_rot, key_rot, value_low], 0)
    heads = lax.all_to_all(packed, "seq", split_axis=2, concat_axis=1, tiled=True)
    query_heads = heads[0].reshape(length, local_heads, HD)
    key_heads = heads[1].reshape(length, local_heads, HD)
    value_heads = heads[2].reshape(length, local_heads, HD)

    def forward_block(index):
        start = index * block
        query_block = lax.dynamic_slice_in_dim(query_heads, start, block, 0)
        scores = (
            jnp.einsum("qhd,khd->hqk", query_block, key_heads, preferred_element_type=jnp.float32)
            * head_scale
        )
        row_top = jnp.max(scores, -1, keepdims=True)
        log_total = row_top + jnp.log(jnp.sum(jnp.exp(scores - row_top), -1, keepdims=True))
        probs = jnp.exp(scores - log_total).astype(jnp.bfloat16)
        attended_block = jnp.einsum(
            "hqk,khd->qhd", probs, value_heads, preferred_element_type=jnp.float32
        )
        return (attended_block.astype(jnp.bfloat16).reshape(block, local_width), log_total[..., 0])

    attended_blocks, log_blocks = lax.map(forward_block, jnp.arange(block_count, dtype=jnp.int32))
    attended_local = attended_blocks.reshape(length, local_width)
    attended = lax.all_to_all(attended_local, "seq", split_axis=0, concat_axis=1, tiled=True)
    resid = tokens + product_t(attended, out_w)
    mlp_normed, mlp_unit, mlp_rstd = norm_forward(resid, mlp_g)
    upper = product_t(mlp_normed, in_w)
    gating = product_t(mlp_normed, gate_w)
    hidden = (gelu_value(upper) * gating).astype(jnp.bfloat16)
    output = (resid + product_t(hidden, down_w)).astype(jnp.bfloat16)
    grad_low = out_grad.reshape(tok_count, D)
    grad_top = grad_low.astype(jnp.float32)
    down_grad = product_tn(grad_low, hidden)
    hidden_grad = jnp.dot(grad_low, down_w, preferred_element_type=jnp.float32)
    upper_grad = (hidden_grad * gating * gelu_slope(upper)).astype(jnp.bfloat16)
    gating_grad = (hidden_grad * gelu_value(upper)).astype(jnp.bfloat16)
    in_grad = product_tn(upper_grad, mlp_normed)
    gate_grad = product_tn(gating_grad, mlp_normed)
    mlp_normed_grad = jnp.dot(upper_grad, in_w, preferred_element_type=jnp.float32) + jnp.dot(
        gating_grad, gate_w, preferred_element_type=jnp.float32
    )
    resid_part, mlp_gain_grad = norm_backward(mlp_normed_grad, mlp_unit, mlp_rstd, mlp_g)
    resid_grad = grad_top + resid_part
    resid_low = resid_grad.astype(jnp.bfloat16)
    out_grad_w = product_tn(resid_low, attended)
    attended_grad = jnp.dot(resid_low, out_w, preferred_element_type=jnp.float32).astype(
        jnp.bfloat16
    )
    grad_local = lax.all_to_all(attended_grad, "seq", split_axis=1, concat_axis=0, tiled=True)
    grad_heads = grad_local.reshape(length, local_heads, HD)
    delta = jnp.sum(
        grad_local.astype(jnp.float32).reshape(length, local_heads, HD)
        * attended_local.astype(jnp.float32).reshape(length, local_heads, HD),
        -1,
    )

    def backward_block(carry, index):
        key_acc, value_acc = carry
        start = index * block
        query_block = lax.dynamic_slice_in_dim(query_heads, start, block, 0)
        grad_block = lax.dynamic_slice_in_dim(grad_heads, start, block, 0)
        delta_block = lax.dynamic_slice_in_dim(delta, start, block, 0).T
        log_total = log_blocks[index]
        scores = (
            jnp.einsum("qhd,khd->hqk", query_block, key_heads, preferred_element_type=jnp.float32)
            * head_scale
        )
        probs = jnp.exp(scores - log_total[..., None])
        probs_low = probs.astype(jnp.bfloat16)
        value_acc = value_acc + jnp.einsum(
            "hqk,qhd->khd", probs_low, grad_block, preferred_element_type=jnp.float32
        )
        prob_grad = jnp.einsum(
            "qhd,khd->hqk", grad_block, value_heads, preferred_element_type=jnp.float32
        )
        score_grad = (probs * (prob_grad - delta_block[..., None]) * head_scale).astype(
            jnp.bfloat16
        )
        query_grad = jnp.einsum(
            "hqk,khd->qhd", score_grad, key_heads, preferred_element_type=jnp.float32
        )
        key_acc = key_acc + jnp.einsum(
            "hqk,qhd->khd", score_grad, query_block, preferred_element_type=jnp.float32
        )
        return ((key_acc, value_acc), query_grad.astype(jnp.bfloat16).reshape(block, local_width))

    empty = jnp.zeros((length, local_heads, HD), jnp.float32)
    (key_acc, value_acc), query_blocks = lax.scan(
        backward_block, (empty, empty), jnp.arange(block_count, dtype=jnp.int32)
    )
    head_grads = jnp.stack(
        [
            query_blocks.reshape(length, local_width),
            key_acc.reshape(length, local_width).astype(jnp.bfloat16),
            value_acc.reshape(length, local_width).astype(jnp.bfloat16),
        ],
        0,
    )
    token_grads = lax.all_to_all(head_grads, "seq", split_axis=1, concat_axis=2, tiled=True)
    query_back = (
        unrotate(token_grads[0].astype(jnp.float32).reshape(tok_count, H, HD), cosine, sine)
        .astype(jnp.bfloat16)
        .reshape(tok_count, D)
    )
    key_back = (
        unrotate(token_grads[1].astype(jnp.float32).reshape(tok_count, H, HD), cosine, sine)
        .astype(jnp.bfloat16)
        .reshape(tok_count, D)
    )
    qkv_grad = jnp.concatenate([query_back, key_back, token_grads[2]], 1)
    qkv_grad_w = product_tn(qkv_grad, attn_normed)
    attn_normed_grad = jnp.dot(qkv_grad, qkv_w, preferred_element_type=jnp.float32)
    input_part, attn_gain_grad = norm_backward(attn_normed_grad, attn_unit, attn_rstd, attn_g)
    input_grad = resid_grad + input_part
    down_final = reduce_weight(down_grad.reshape(owners, out_rows, owners * ff_rows), 0)
    in_final = reduce_weight(in_grad.reshape(owners, ff_rows, D), 1)
    gate_final = reduce_weight(gate_grad.reshape(owners, ff_rows, D), 1)
    out_final = reduce_weight(out_grad_w.reshape(owners, out_rows, D), 1)
    gain_grads = jnp.concatenate(
        [attn_gain_grad.reshape(owners, gain_rows), mlp_gain_grad.reshape(owners, gain_rows)], 1
    )[:, None, :]
    gain_grads = jnp.pad(gain_grads, ((0, 0), (0, 15), (0, D - 2 * gain_rows)))
    last = reduce_weight(
        jnp.concatenate([qkv_grad_w.reshape(owners, qkv_rows, D), gain_grads], 1), 1
    )
    qkv_final = last[:qkv_rows]
    attn_gain_final = last[qkv_rows, :gain_rows]
    mlp_gain_final = last[qkv_rows, gain_rows : 2 * gain_rows]
    return (
        output.reshape(1, tok_count, D),
        input_grad.reshape(1, tok_count, D),
        attn_gain_final,
        qkv_final,
        out_final,
        mlp_gain_final,
        in_final,
        gate_final,
        down_final,
    )


def solution(mesh):
    in_specs = (
        P("fsdp", "seq", None),
        P("fsdp"),
        P("fsdp", None),
        P("fsdp", None),
        P("fsdp"),
        P("fsdp", None),
        P("fsdp", None),
        P("fsdp", None),
        P("fsdp", "seq", None),
    )
    out_specs = (
        P("fsdp", "seq", None),
        P("fsdp", "seq", None),
        P("fsdp"),
        P("fsdp", None),
        P("fsdp", None),
        P("fsdp"),
        P("fsdp", None),
        P("fsdp", None),
        P("fsdp", None),
    )
    return jax.shard_map(
        on_device, mesh=mesh, in_specs=in_specs, out_specs=out_specs, check_vma=False
    )
```
